256 devices in a mesh: rep: 8 (over z), fsdp: 32 (over y, x, core).
Axes of the slice: x: 4, y: 4, z: 8, core: 2. Of those that a mesh axis runs over, the one named last changes fastest.
Arguments:
- tokens: bfloat16 [65536, 4096], P(('rep', 'fsdp')), may hold values from -6 to 6
- out_grad: bfloat16 [65536, 14336], P(('rep', 'fsdp')), may hold values from -6 to 6
- weight_blocks: bfloat16 [256, 128, 128], P('fsdp'), may hold values from -0.1875 to 0.1875
- block_row: int32 [256], replicated, may hold values from 0 to 31, as said below
- block_col: int32 [256], replicated, may hold values from 0 to 111
- send_list: int32 [32, 8, 3], P('fsdp'), may hold values from 0 to 8, as said below
Outputs:
- token_grad: bfloat16 [65536, 4096], P(('rep', 'fsdp'))
- grad_owned: float32 [8, 32, 3, 128, 128], P('rep', 'fsdp')
The draws below stay inside these ranges and needn't reach their ends.
Inputs may be any that keep to these rules, and one draw needn't show every extreme that they name: The pairs (block_row[k], block_col[k]) are all distinct. For each f, every local block number 0 to 7 stands exactly once in send_list[f] over all owners and slots, in increasing order within an owner's slots, followed by the pad value 8; for each f some owner fills all 3 slots.
All inputs are finite; a program needn't handle non-finite values.
Results may differ from the reference program's by a relative error of at most 0.001.
Values may be sent and summed in bfloat16 or wider, within the bound.
No kernel may reach another device: no remote copies, remote signals or barrier semaphores. Data moves between devices by JAX's collectives and lax.ppermute only.
A program may use at most 256 MiB of HBM per device.

```python
import jax
import jax.numpy as jnp
from jax import lax

D = 4096
FF = 14336
BS = 128
BLK_DEV = 8
CAP = 3
TOKENS = 65536
NNZ = 256
N_REP = 8
N_FSDP = 32


def pattern(key):
    base_key = jax.random.fold_in(key, 7)
    first_key, second_key = jax.random.split(base_key)
    row_total = D // BS
    col_total = FF // BS
    serial = jnp.arange(NNZ, dtype=jnp.int32)
    shifts = jax.random.randint(first_key, (row_total,), 0, col_total).astype(jnp.int32)
    shifts = shifts.at[0].set(col_total - 1)
    row_raw = serial % row_total
    col_raw = (serial // row_total + shifts[row_raw]) % col_total
    shuffle = jax.random.permutation(second_key, NNZ)
    return (row_raw[shuffle].astype(jnp.int32), col_raw[shuffle].astype(jnp.int32))


def draw_block_row(key, part):
    return pattern(key)[0]


def draw_block_col(key, part):
    return pattern(key)[1]


def draw_send_list(key, part):

    def one_shard(shard_key):
        first_key, second_key = jax.random.split(shard_key)
        busiest = jax.random.randint(first_key, (), 0, N_REP).astype(jnp.int32)
        position = jax.random.permutation(second_key, BLK_DEV).astype(jnp.int32)
        others = (busiest + 1 + (position - CAP) % (N_REP - 1)) % N_REP
        owners = jnp.where(position < CAP, busiest, others).astype(jnp.int32)
        peers = jnp.arange(N_REP, dtype=jnp.int32)
        local_ids = jnp.arange(BLK_DEV, dtype=jnp.int32)
        sort_keys = (owners[None, :] != peers[:, None]).astype(jnp.int32) * BLK_DEV + local_ids[None, :]
        ranked = jnp.argsort(sort_keys, axis=1)[:, :CAP].astype(jnp.int32)
        matches = owners[ranked] == peers[:, None]
        return jnp.where(matches, ranked, BLK_DEV).astype(jnp.int32)
    shard_keys = jax.random.split(jax.random.fold_in(key, 11), N_FSDP)
    return jax.vmap(one_shard)(shard_keys)


def level_of(own_key, shape, cuts, smallest, top_value):
    factor_of, own = 1.0, jax.random.fold_in(own_key, 6)
    for dim, parts in cuts:
        steps = jnp.exp(jax.random.uniform(jax.random.fold_in(own, dim), (parts,), jnp.float32, smallest / len(cuts), top_value / len(cuts)))
        factor_of = factor_of * jnp.repeat(steps, shape[dim] // parts).reshape([-1 if axis == dim else 1 for axis in range(len(shape))])
    return factor_of


def bell_draw(stream_key, extent, width, bound, shards=(), kind=jnp.bfloat16):
    result = jax.random.normal(stream_key, extent, jnp.float32) * width
    if len(shards) > 0:
        result = level_of(stream_key, extent, shards, -0.22, 0.18) * result
    return jnp.clip(result, min=-bound, max=bound).astype(kind)


def setup_inputs(seed: int = 0) -> dict:
    arg_keys = jax.random.split(jax.random.key(seed), 7)
    tokens = bell_draw(arg_keys[0], (TOKENS, D), 1.0, 6.0, ((0, 256),))
    out_grad = bell_draw(arg_keys[1], (TOKENS, FF), 1.0, 6.0, ((0, 256),))
    weight_blocks = bell_draw(arg_keys[2], (NNZ, BS, BS), (NNZ * BS // (D // BS)) ** -0.5, 0.1875, ((0, 32),))
    block_row = draw_block_row(jax.random.fold_in(arg_keys[6], 71), 0)
    block_col = draw_block_col(jax.random.fold_in(arg_keys[6], 71), 0)
    send_list = draw_send_list(jax.random.fold_in(arg_keys[6], 71), 0)
    return {"tokens": tokens, "out_grad": out_grad, "weight_blocks": weight_blocks, "block_row": block_row, "block_col": block_col, "send_list": send_list}


def reference(tokens, out_grad, weight_blocks, block_row, block_col, send_list):
    def input_step(running, block_index):
        row_start = block_row[block_index] * BS
        col_start = block_col[block_index] * BS
        columns = lax.dynamic_slice_in_dim(out_grad, col_start, BS, 1).astype(jnp.float32)
        weight = weight_blocks[block_index].astype(jnp.float32)
        update = jnp.dot(columns, weight.T, precision=lax.Precision.HIGHEST)
        current = lax.dynamic_slice_in_dim(running, row_start, BS, 1)
        return lax.dynamic_update_slice_in_dim(running, current + update, row_start, 1), None

    zero_grad = jnp.zeros((TOKENS, D), jnp.float32)
    summed, unused = lax.scan(input_step, zero_grad, jnp.arange(NNZ, dtype=jnp.int32))
    token_grad = summed.astype(jnp.bfloat16)

    def weight_step(block_index):
        row_start = block_row[block_index] * BS
        col_start = block_col[block_index] * BS
        left_cols = lax.dynamic_slice_in_dim(tokens, row_start, BS, 1).astype(jnp.float32)
        right_cols = lax.dynamic_slice_in_dim(out_grad, col_start, BS, 1).astype(jnp.float32)
        return jnp.dot(left_cols.T, right_cols, precision=lax.Precision.HIGHEST)

    block_grad = lax.map(weight_step, jnp.arange(NNZ, dtype=jnp.int32)) * (TOKENS ** -0.5)
    padded = jnp.concatenate([block_grad, jnp.zeros((1, BS, BS), jnp.float32)], axis=0)
    shard_base = (jnp.arange(N_FSDP, dtype=jnp.int32) * BLK_DEV)[:, None, None]
    global_index = jnp.where(send_list < BLK_DEV, shard_base + send_list, NNZ).astype(jnp.int32)
    owned_blocks = jnp.take(padded, global_index, axis=0)
    return token_grad, jnp.transpose(owned_blocks, (1, 0, 2, 3, 4))
```

```python
import functools

import jax
import jax.numpy as jnp
from jax import lax
from jax.experimental import pallas as pl
from jax.experimental.pallas import tpu as pltpu
from jax.sharding import PartitionSpec as P


SIDE = 4
CORES = 2
BS = 128
SIDEBAND = 16
PAIR = 2 * BS + SIDEBAND
UNITS = 16
UNROLL = 2
TOP = 8192.0
TINY = 1e-33
VMEM = pl.BlockSpec(memory_space=pltpu.VMEM)
SMEM = pl.BlockSpec(memory_space=pltpu.SMEM)


def fast(a):
    return pltpu.with_memory_space_constraint(a, pltpu.VMEM)


def encode(blocks, ref, base):
    grouped = [b.reshape(BS // SIDEBAND, SIDEBAND, BS) for b in blocks]
    largest = functools.reduce(jnp.maximum, [jnp.max(jnp.abs(g), axis=0) for g in grouped])
    side = largest.astype(jnp.bfloat16)
    top = side.astype(jnp.float32)
    scale = jnp.where(top > TINY, TOP / jnp.maximum(top, TINY), 0.0)
    for i, g in enumerate(grouped):
        u = g * scale[None]
        u2 = u * u
        u4 = u2 * u2
        y = (u4 * u4) * u
        ref[pl.ds(base + i * BS, BS), :] = y.reshape(BS, BS).astype(jnp.bfloat16)
    ref[pl.ds(base + len(blocks) * BS, SIDEBAND), :] = side


def decode(ref, base, count):
    side = ref[pl.ds(base + count * BS, SIDEBAND), :].astype(jnp.float32) * (1.0 / TOP)
    out = []
    for i in range(count):
        y = ref[pl.ds(base + i * BS, BS), :].astype(jnp.float32)
        r = jnp.exp2(jnp.log2(jnp.abs(y)) * (1.0 / 9.0))
        r = jnp.where(y < 0, -r, r).reshape(BS // SIDEBAND, SIDEBAND, BS)
        out.append((r * side[None]).reshape(BS, BS))
    return out


def place(me):
    core = lax.rem(me, CORES)
    chip = lax.div(me, CORES)
    return lax.div(chip, SIDE), lax.rem(chip, SIDE), core


def block_of(half, y, x, step, u):
    other = lax.div(u, 4)
    yy = jnp.where(half == 0, lax.rem(y + step, SIDE), other)
    xx = jnp.where(half == 0, other, lax.rem(x + step, SIDE))
    core = lax.rem(lax.div(u, 2), 2)
    return ((yy * SIDE + xx) * CORES + core) * 8 + half * 4 + lax.rem(u, 2) * 2


def product(tok, grad, row, col, k):
    left = tok[pl.ds(pl.multiple_of(row[k] * BS, BS), BS), :]
    right = grad[:, pl.ds(pl.multiple_of(col[k] * BS, BS), BS)]
    return jnp.dot(left, right, preferred_element_type=jnp.float32)


def first_kernel(steps, row, col, where, tok, grad, out):
    y, x, core = place(where[0])
    for n, step in enumerate(steps):

        def body(u, _, n=n, step=step):
            k = block_of(1 - core, y, x, step, u)
            vs = [product(tok, grad, row, col, k + i) for i in range(2)]
            encode(vs, out, pl.multiple_of((n * UNITS + u) * PAIR, 16))
            return 0

        lax.fori_loop(0, UNITS, body, 0, unroll=UNROLL)


def second_kernel(steps, row, col, where, tok, grad, recv, *rest):
    y, x, core = place(where[0])
    half_units = UNITS // 2

    def run(n, step, first, out, relay):
        def body(i, _):
            u = first + i
            k = block_of(core, y, x, step, u)
            got = decode(recv, pl.multiple_of((n * UNITS + u) * PAIR, 16), 2)
            vs = [product(tok, grad, row, col, k + i) + got[i] for i in range(2)]
            if relay is not None:
                more = decode(relay, pl.multiple_of(i * PAIR, 16), 2)
                vs = [a + b for a, b in zip(vs, more)]
            at = u if step != 2 else i
            if step:
                encode(vs, out, pl.multiple_of(at * PAIR, 16))
            else:
                for j in range(2):
                    out[pl.ds(pl.multiple_of((at * 2 + j) * BS, BS), BS), :] = vs[j]
            return 0

        lax.fori_loop(0, half_units, body, 0, unroll=UNROLL)

    if steps == (2,):
        run(0, 2, 0, rest[0], None)
        run(0, 2, half_units, rest[1], None)
    elif steps == (0,):
        run(0, 0, 0, rest[0], None)
        run(0, 0, half_units, rest[0], None)
    else:
        from_back, from_front, on, back = rest
        run(0, 1, half_units, on, None)
        run(1, 3, 0, back, None)
        run(0, 1, 0, on, from_back)
        run(1, 3, half_units, back, from_front)


def third_kernel(where, own, r1, r3, m1, m2, m3, keep):
    y, x, core = place(where[0])
    here = jnp.where(core == 0, x, y)
    for step, out in ((2, m2), (1, m1), (3, m3), (0, keep)):

        def body(n, _, step=step, out=out):
            u = lax.rem(here + step, SIDE) * 4 + n
            base = pl.multiple_of(u * PAIR, 16)
            got = [decode(r, base, 2) for r in (r1, r3)]
            vs = []
            for i in range(2):
                v = own[pl.ds(pl.multiple_of((u * 2 + i) * BS, BS), BS), :]
                vs.append(v + (got[0][i] + got[1][i]))
            if step:
                encode(vs, out, pl.multiple_of(n * PAIR, 16))
            else:
                for i in range(2):
                    out[pl.ds(pl.multiple_of((n * 2 + i) * BS, BS), BS), :] = vs[i]
            return 0

        lax.fori_loop(0, 4, body, 0, unroll=2)


def plane_kernel(where, own, r1, r2, r3, mine, other):
    _, _, core = place(where[0])
    for cc, out in ((core, mine), (1 - core, other)):
        for jp in range(2):
            u = cc * 2 + jp
            got = [decode(r, pl.multiple_of(u * PAIR, 16), 2) for r in (r1, r2, r3)]
            for i in range(2):
                v = own[pl.ds(pl.multiple_of((u * 2 + i) * BS, BS), BS), :]
                out[jp * 2 + i] = v + (got[0][i] + got[1][i]) + got[2][i]


def fourth_kernel(reps, slots, where, lists, mine, other, keep, out, sums):
    z = where[1]
    _, _, core = place(where[0])
    for i in range(4):
        sums[core * 4 + i] = mine[i]
        sums[(1 - core) * 4 + i] = other[i]
    sums[8] = jnp.zeros((BS, BS), jnp.float32)

    def body(p, _):
        encode([sums[lists[p * slots + t]] for t in range(slots)], out.at[p], 0)
        return 0

    lax.fori_loop(0, reps, body, 0, unroll=2)
    for t in range(slots):
        keep[pl.ds(t * BS, BS), :] = sums[lists[z * slots + t]]


def fifth_kernel(scale, reps, slots, where, own, recv, out):
    for t in range(slots):
        out[t] = own[pl.ds(t * BS, BS), :]

    def body(shift, _):
        got = decode(recv.at[lax.rem(where[1] + shift, reps)], 0, slots)
        for t in range(slots):
            out[t] += got[t]
        return 0

    lax.fori_loop(1, reps, body, 0)
    for t in range(slots):
        out[t] = out[t] * scale


def token_kernel(row, col, where, grad, *rest):
    pieces, out, acc = rest[:-2], rest[-2], rest[-1]
    y, x, core = place(where[0])
    acc[...] = jnp.zeros_like(acc)
    for n, piece in enumerate(pieces):
        half = core if n < 5 else 1 - core
        back, first = ((0, 0), (1, 0), (3, 0), (2, 0), (2, 4 * SIDE))[n % 5]

        def body(at, _, piece=piece, half=half, back=back, first=first):
            i = first + at
            other = lax.div(i, 8)
            yy = jnp.where(half == 0, back, other)
            xx = jnp.where(half == 0, other, back)
            chip = lax.rem(y + SIDE - yy, SIDE) * SIDE + lax.rem(x + SIDE - xx, SIDE)
            owner = lax.rem(half + lax.rem(lax.div(i, 4), 2), 2)
            k = (chip * CORES + owner) * 8 + half * 4 + lax.rem(i, 4)
            left = grad[:, pl.ds(pl.multiple_of(col[k] * BS, BS), BS)]
            part = lax.dot_general(
                left,
                piece[pl.ds(pl.multiple_of(at * BS, BS), BS), :],
                (((1,), (1,)), ((), ())),
                preferred_element_type=jnp.float32,
            )
            acc[:, pl.ds(pl.multiple_of(row[k] * BS, BS), BS)] += part
            return 0

        lax.fori_loop(0, piece.shape[0] // BS, body, 0, unroll=4)
    out[...] = acc[...].astype(jnp.bfloat16)


def call(kernel, in_specs, outs, *args, scratch=(), flops=0, moved=0, limit=16):
    return pl.pallas_call(
        kernel,
        in_specs=in_specs,
        out_specs=[VMEM] * len(outs),
        out_shape=outs,
        scratch_shapes=list(scratch),
        compiler_params=pltpu.CompilerParams(vmem_limit_bytes=limit * 1024 * 1024),
        cost_estimate=pl.CostEstimate(flops=flops, bytes_accessed=moved, transcendentals=0),
    )(*args)


def move(a, axis, pairs):
    return lax.ppermute(a, axis, pairs)


def work(tokens, out_grad, weight_blocks, block_row, block_col, send_list):
    fsdp = lax.axis_size("fsdp")
    reps = lax.axis_size("rep")
    slots = send_list.shape[2]
    rows_here = tokens.shape[0]
    nnz = block_row.shape[0]
    scale = float(rows_here * reps * fsdp) ** -0.5
    where = jnp.stack([lax.axis_index("fsdp"), lax.axis_index("rep")]).astype(jnp.int32)

    def ring(first, step):
        pairs = []
        for f in range(fsdp):
            y, x, c = f // (SIDE * CORES), f // CORES % SIDE, f % CORES
            dy, dx = (step, 0) if (c == 0) == first else (0, step)
            to = ((y + dy) % SIDE * SIDE + (x + dx) % SIDE) * CORES + c
            pairs.append((f, to))
        return pairs

    swap = [(f, f ^ 1) for f in range(fsdp)]
    group_shape = jax.ShapeDtypeStruct((UNITS * PAIR, BS), jnp.bfloat16)
    kept_shape = jax.ShapeDtypeStruct((UNITS * 2 * BS, BS), jnp.float32)

    core = lax.rem(lax.axis_index("fsdp"), CORES)
    flat = weight_blocks.reshape(8 * BS, BS)
    stay = lax.dynamic_slice_in_dim(flat, core * 4 * BS, 4 * BS, 0)
    leave = lax.dynamic_slice_in_dim(flat, (1 - core) * 4 * BS, 4 * BS, 0)
    part = jnp.concatenate([stay, move(leave, "fsdp", swap)], axis=0)
    along = [part] + [move(part, "fsdp", ring(False, s)) for s in (1, 2, 3)]
    along = jnp.concatenate(along, axis=0)
    back, front = (move(along, "fsdp", ring(True, s)) for s in (1, 3))
    middle = along.shape[0] // 2
    far = [move(back[:middle], "fsdp", ring(True, 1)), move(front[middle:], "fsdp", ring(True, 3))]
    pieces = [along, back, front, *far]
    pieces += [move(p, "fsdp", swap) for p in pieces]

    tok = fast(tokens.T)
    grad = fast(out_grad)
    flops = 2 * rows_here * BS * BS * 32
    order = ((2,), (1, 3), (0,))
    arrived = []
    for steps in order:
        mine = call(
            functools.partial(first_kernel, steps),
            [SMEM, SMEM, SMEM, VMEM, VMEM],
            [jax.ShapeDtypeStruct((len(steps) * UNITS * PAIR, BS), jnp.bfloat16)],
            block_row, block_col, where, tok, grad,
            flops=flops * len(steps),
        )[0]
        arrived.append(move(mine, "fsdp", swap))
    half_shape = jax.ShapeDtypeStruct((UNITS // 2 * PAIR, BS), jnp.bfloat16)

    def second(i, outs, *more):
        steps = order[i]
        return call(
            functools.partial(second_kernel, steps),
            [SMEM, SMEM, SMEM] + [VMEM] * (3 + len(more)),
            outs,
            block_row, block_col, where, tok, grad, arrived[i], *more,
            flops=flops * len(steps),
        )

    on, behind = second(0, [half_shape] * 2)
    from_back = move(on, "fsdp", ring(True, 1))
    from_front = move(behind, "fsdp", ring(True, 3))
    (kept,) = second(2, [kept_shape])
    on, behind = second(1, [group_shape] * 2, from_back, from_front)
    recv = {1: move(on, "fsdp", ring(True, 1)), 3: move(behind, "fsdp", ring(True, 3))}
    small = jax.ShapeDtypeStruct((4 * PAIR, BS), jnp.bfloat16)
    m1, m2, m3, keep = call(
        third_kernel,
        [SMEM] + [VMEM] * 3,
        [small] * 3 + [jax.ShapeDtypeStruct((8 * BS, BS), jnp.float32)],
        where, kept, recv[1], recv[3],
    )
    got = {s: move(m, "fsdp", ring(False, s)) for s, m in ((2, m2), (1, m1), (3, m3))}
    mine, other = call(
        plane_kernel,
        [SMEM] + [VMEM] * 4,
        [jax.ShapeDtypeStruct((4, BS, BS), jnp.float32)] * 2,
        where, keep, got[1], got[2], got[3],
    )
    other = move(other, "fsdp", swap)
    zrows = slots * BS + SIDEBAND
    keep, outgoing = call(
        functools.partial(fourth_kernel, reps, slots),
        [SMEM, SMEM] + [VMEM] * 2,
        [
            jax.ShapeDtypeStruct((slots * BS, BS), jnp.float32),
            jax.ShapeDtypeStruct((reps, zrows, BS), jnp.bfloat16),
        ],
        where, send_list.reshape(-1), mine, other,
        scratch=[pltpu.VMEM((9, BS, BS), jnp.float32)],
    )
    incoming = lax.all_to_all(outgoing, "rep", split_axis=0, concat_axis=0, tiled=True)
    token_grad = call(
        token_kernel,
        [SMEM, SMEM, SMEM] + [VMEM] * 11,
        [jax.ShapeDtypeStruct(tokens.shape, jnp.bfloat16)],
        block_row, block_col, where, grad, *pieces,
        scratch=[pltpu.VMEM(tokens.shape, jnp.float32)],
        flops=2 * rows_here * BS * BS * nnz,
        limit=20,
    )[0]
    incoming, token_grad = lax.optimization_barrier((incoming, token_grad))
    grad_owned = call(
        functools.partial(fifth_kernel, scale, reps, slots),
        [SMEM, VMEM, VMEM],
        [jax.ShapeDtypeStruct((slots, BS, BS), jnp.float32)],
        where, keep, incoming,
    )[0]
    return token_grad, grad_owned[None, None]


def solution(mesh):
    return jax.shard_map(
        work,
        mesh=mesh,
        in_specs=(
            P(("rep", "fsdp"), None),
            P(("rep", "fsdp"), None),
            P("fsdp", None, None),
            P(),
            P(),
            P("fsdp", None, None),
        ),
        out_specs=(P(("rep", "fsdp"), None), P("rep", "fsdp", None, None, None)),
        check_vma=False,
    )
```
